32 devices in a mesh: feat: 4 (over y, x), sect: 2 (over core), rep: 4 (over z).
Axes of the slice: x: 2, y: 2, z: 4, core: 2. Of those that a mesh axis runs over, the one named last changes fastest.
Arguments:
- features: bfloat16 [4, 768, 16384], P('rep', 'feat', 'sect'), may hold values from -6 to 6
- w_first: bfloat16 [768, 256], P('feat'), may hold values from -0.21875 to 0.21875
- w_upper: bfloat16 [256, 256], replicated, may hold values from -0.375 to 0.375
- cotangent: bfloat16 [4, 256, 256], P('rep', ('feat', 'sect')), may hold values from -6 to 6
- tile_rows: int32 [4, 128], P('rep', 'sect'), may hold values from 0 to 1, as said below
- tile_cols: int32 [4, 128], P('rep', 'sect'), may hold values from 0 to 63, as said below
- tile_count: int32 [4, 2], P('rep', 'sect'), may hold values from 8 to 64, as said below
- tile_vals: bfloat16 [4, 128, 128, 128], P('rep', 'sect'), may hold values from -0.0625 to 0.0625
Outputs:
- hid_grad: bfloat16 [4, 256, 256], P('rep', ('feat', 'sect'))
- grad_first: float32 [768, 256], P('feat')
- grad_upper: float32 [256, 256], replicated
The draws below stay inside these ranges and needn't reach their ends.
Inputs may be any that keep to these rules, and one draw needn't show every extreme that they name: `tile_count`: live slots of each replica and sect index; in every draw one of them holds exactly 64 and another exactly 8. `tile_rows`: within one replica and sect index the live slots name distinct (row, column) block pairs; slots at or past the count hold 0 in both id arrays and their tile_vals are to be ignored. `tile_cols`: block of 128 source nodes among the sect index's own 64 blocks.
All inputs are finite; a program needn't handle non-finite values.
Results may differ from the reference program's by a relative error of at most 0.017.
Values may be sent and summed in bfloat16 or wider, within the bound.
A program may use at most 64 MiB of HBM per device.

```python
import math
import jax
import jax.numpy as jnp
from jax import lax

F = 768
H = 256
TILE = 128
SRC_BLK_DEV = 64
MAXT = 64
DST = 256
DST_BLK = 2
SRC = 16384
N_SECT = 2
N_REP = 4


def tile_plan(key):
    pair_total = DST_BLK * SRC_BLK_DEV
    group_total = N_REP * N_SECT
    base = jax.random.fold_in(key, 7)
    lowest = MAXT // 8
    uniform_draw = jax.random.randint(jax.random.fold_in(base, 1), (group_total,), 0, 1000)
    counts = lowest + (MAXT - lowest) * uniform_draw * uniform_draw // 1000000
    first_pick = jax.random.randint(jax.random.fold_in(base, 2), (), 0, group_total)
    second_pick = (first_pick + 1 + jax.random.randint(jax.random.fold_in(base, 3), (), 0, group_total - 1)) % group_total
    position = jnp.arange(group_total)
    counts = jnp.where(position == first_pick, MAXT, jnp.where(position == second_pick, lowest, counts))
    subkeys = jax.random.split(jax.random.fold_in(base, 4), group_total)
    orders = jax.vmap(lambda subkey: jax.random.permutation(subkey, pair_total)[:MAXT])(subkeys)
    live_slot = jnp.arange(MAXT)[None, :] < counts[:, None]
    row_block = jnp.where(live_slot, orders // SRC_BLK_DEV, 0)
    column_block = jnp.where(live_slot, orders % SRC_BLK_DEV, 0)
    return (row_block.reshape(N_REP, N_SECT * MAXT).astype(jnp.int32), column_block.reshape(N_REP, N_SECT * MAXT).astype(jnp.int32), counts.reshape(N_REP, N_SECT).astype(jnp.int32))


def draw_tile_rows(key, part):
    return tile_plan(key)[0]


def draw_tile_cols(key, part):
    return tile_plan(key)[1]


def draw_tile_count(key, part):
    return tile_plan(key)[2]


def steps_of(stream_key, dims, pieces, least, high):
    def one(dim, parts):
        draws = jax.random.uniform(jax.random.fold_in(jax.random.fold_in(stream_key, 6), dim), (parts,), jnp.float32, least / len(pieces), high / len(pieces))
        return jnp.repeat(jnp.exp(draws), dims[dim] // parts).reshape((-1,) + (1,) * (len(dims) - dim - 1))

    factor_of = one(*pieces[0])
    for cut in pieces[1:]:
        factor_of = factor_of * one(*cut)
    return factor_of


def bell_draw(own_key, extent, spread, bound, cuts=(), kind=jnp.bfloat16):
    drawn = spread * jax.random.normal(own_key, extent, jnp.float32)
    if cuts:
        drawn = drawn * steps_of(own_key, extent, cuts, -0.22, 0.18)
    return jnp.clip(drawn, -bound, bound).astype(kind)


def setup_inputs(seed: int = 0) -> dict:
    streams_of = jax.random.split(jax.random.key(seed), 9)
    features = bell_draw(streams_of[0], (N_REP, F, SRC), 1.0, 6.0, ((0, 4), (1, 4), (2, 2)))
    w_first = bell_draw(streams_of[1], (F, H), F ** -0.5, 0.21875, ((0, 4),))
    w_upper = bell_draw(streams_of[2], (H, H), H ** -0.5, 0.375)
    cotangent = bell_draw(streams_of[3], (N_REP, DST, H), 1.0, 6.0, ((0, 4), (1, 8)))
    tile_rows = draw_tile_rows(jax.random.fold_in(streams_of[8], 71), 0)
    tile_cols = draw_tile_cols(jax.random.fold_in(streams_of[8], 71), 0)
    tile_count = draw_tile_count(jax.random.fold_in(streams_of[8], 71), 0)
    tile_vals = bell_draw(streams_of[7], (N_REP, N_SECT * MAXT, TILE, TILE), (TILE * max(1, MAXT * N_SECT // DST_BLK)) ** -0.5, 0.0625, ((0, 4), (1, 2)))
    return {"features": features, "w_first": w_first, "w_upper": w_upper, "cotangent": cotangent, "tile_rows": tile_rows, "tile_cols": tile_cols, "tile_count": tile_count, "tile_vals": tile_vals}


def reference(features, w_first, w_upper, cotangent, tile_rows, tile_cols, tile_count, tile_vals):
    slot_index = jnp.arange(N_SECT * MAXT, dtype=jnp.int32)
    section = (slot_index // MAXT).astype(jnp.int32)

    def per_replica(inputs):
        feats, upstream_in, row_block, column_block, counts, weights_tile = inputs
        projected = lax.dot_general(feats, w_first, (((0,), (0,)), ((), ())), preferred_element_type=jnp.float32).astype(jnp.bfloat16)
        live_slot = slot_index % MAXT < counts[section]
        global_col = (section * SRC_BLK_DEV + column_block).astype(jnp.int32)
        blocks = projected.reshape(N_SECT * SRC_BLK_DEV, TILE, H)[global_col]
        products = jnp.einsum('trc,tch->trh', weights_tile.astype(jnp.float32), blocks.astype(jnp.float32))
        products = products * live_slot[:, None, None].astype(jnp.float32)
        aggregate = jnp.zeros((DST_BLK, TILE, H), jnp.float32).at[row_block].add(products).reshape(DST, H)
        activated = jax.nn.silu(aggregate).astype(jnp.bfloat16)
        upstream = jnp.dot(upstream_in, w_upper.T, preferred_element_type=jnp.float32)
        gate_sigmoid = jax.nn.sigmoid(aggregate)
        hidden_grad = (upstream * gate_sigmoid * (1.0 + aggregate * (1.0 - gate_sigmoid))).astype(jnp.bfloat16)
        upper_part = lax.dot_general(activated, upstream_in, (((0,), (0,)), ((), ())), preferred_element_type=jnp.float32)
        picked = hidden_grad.reshape(DST_BLK, TILE, H)[row_block].astype(jnp.float32)
        backward = jnp.einsum('trc,trh->tch', weights_tile.astype(jnp.float32), picked)
        backward = backward * live_slot[:, None, None].astype(jnp.float32)
        source_grad = jnp.zeros((N_SECT * SRC_BLK_DEV, TILE, H), jnp.float32).at[global_col].add(backward).reshape(SRC, H)
        source_grad = source_grad.astype(jnp.bfloat16)
        first_part = jnp.dot(feats, source_grad, preferred_element_type=jnp.float32)
        return (hidden_grad, first_part, upper_part)
    hid_grad, first_parts, upper_parts = lax.map(per_replica, (features, cotangent, tile_rows, tile_cols, tile_count, tile_vals))
    first_scale = 1.0 / math.sqrt(N_REP * N_SECT * MAXT * TILE)
    upper_scale = 1.0 / math.sqrt(N_REP * DST)
    grad_first = lax.optimization_barrier(jnp.sum(first_parts, axis=0)) * first_scale
    grad_upper = lax.optimization_barrier(jnp.sum(upper_parts, axis=0)) * upper_scale
    return (hid_grad, grad_first, grad_upper)
```

```python
import functools
import math

import jax
import jax.numpy as jnp
from jax import lax
from jax.experimental import pallas as pl
from jax.experimental.pallas import tpu as pltpu
from jax.sharding import PartitionSpec as P

MESH = pl.DeviceIdType.MESH
F32 = jnp.float32
BF16 = jnp.bfloat16
NT = (((1,), (1,)), ((), ()))
TN = (((0,), (0,)), ((), ()))
X_CHUNKS = 4


def mix_kernel(rows, cols, count, x_hbm, tiles_hbm, b_ref, dense, x_buf, x_sem, tile_sem):
    tile = tiles_hbm.shape[1]
    src = x_buf.shape[1]
    step = src // X_CHUNKS

    def x_copy(i):
        lanes = pl.ds(i * step, step)
        return pltpu.make_async_copy(x_hbm.at[:, lanes], x_buf.at[:, lanes], x_sem.at[i])

    for i in range(X_CHUNKS):
        x_copy(i).start()
    dense[...] = jnp.zeros_like(dense)

    def tile_copy(j):
        r = pl.multiple_of(rows[j] * tile, tile)
        c = pl.multiple_of(cols[j] * tile, tile)
        return pltpu.make_async_copy(
            tiles_hbm.at[j], dense.at[pl.ds(r, tile), pl.ds(c, tile)], tile_sem.at[j]
        )

    live = count[0]

    def start(j, carry):
        tile_copy(j).start()
        return carry

    def finish(j, carry):
        tile_copy(j).wait()
        return carry

    lax.fori_loop(0, live, start, 0)
    lax.fori_loop(0, live, finish, 0)
    total = None
    for i in range(X_CHUNKS):
        x_copy(i).wait()
        lanes = pl.ds(i * step, step)
        part = lax.dot_general(dense[:, lanes], x_buf[:, lanes], NT, preferred_element_type=F32)
        total = part if total is None else total + part
    b_ref[...] = total.astype(BF16)


def exchange_kernel(
    axes, sizes, b_ref, wf_ref, wu_ref, cot_ref, hid_ref, gf_ref, gu_ref,
    cot_all, agg_out, agg_in, hid_all, act_all, b_in, gf_z, gu_z, gf_halves, gu_all,
    cot_s, cot_r, agg_s, agg_r, hid_s, hid_r, act_s, act_r, b_s, b_r,
    gfz_s, gfz_r, guz_s, guz_r, gfh_s, gfh_r, gua_s, gua_r,
):
    feats, sects, reps = sizes
    plane = feats * sects
    pos = {"feat": lax.axis_index("feat"), "sect": lax.axis_index("sect"), "rep": lax.axis_index("rep")}
    core = pos["sect"]
    me = pos["feat"] * sects + core
    z = pos["rep"]
    own, width = cot_ref.shape
    half = width // sects

    def dev(**changes):
        at = dict(pos, **changes)
        return tuple(at[a] for a in axes)

    def in_plane(k):
        q = (me + k) % plane
        return q, dev(feat=q // sects, sect=q % sects)

    def before(k):
        return (me + plane - k) % plane

    def in_z(k):
        q = (z + k) % reps
        return q, dev(rep=q)

    def before_z(k):
        return (z + reps - k) % reps

    partner = dev(sect=(core + 1) % sects)

    def remote(src, dst, s, r, to):
        return pltpu.make_async_remote_copy(
            src_ref=src, dst_ref=dst, send_sem=s, recv_sem=r, device_id=to, device_id_type=MESH
        )

    barrier = pltpu.get_barrier_semaphore()
    for k in range(1, plane):
        pl.semaphore_signal(barrier, inc=1, device_id=in_plane(k)[1], device_id_type=MESH)
    for k in range(1, reps):
        pl.semaphore_signal(barrier, inc=1, device_id=in_z(k)[1], device_id_type=MESH)
    b16 = b_ref[...]
    part = lax.dot_general(b16, wf_ref[...], (((1,), (0,)), ((), ())), preferred_element_type=F32)
    agg_out[...] = part.astype(BF16).reshape(agg_out.shape)
    cot_all[me] = cot_ref[...]
    pl.semaphore_wait(barrier, plane + reps - 2)

    sent = []
    for k in range(1, plane):
        q, to = in_plane(k)
        c = remote(agg_out.at[q], agg_in.at[k], agg_s.at[k], agg_r.at[k], to)
        c.start()
        sent.append(c)
    for k in range(1, plane):
        c = remote(cot_ref, cot_all.at[me], cot_s.at[k], cot_r.at[k], in_plane(k)[1])
        c.start()
        sent.append(c)
    b_copy = remote(b_ref, b_in, b_s, b_r, partner)
    b_copy.start()

    upstream = lax.dot_general(cot_ref[...], wu_ref[...], NT, preferred_element_type=F32)
    agg = agg_out[me].astype(F32)
    for k in range(1, plane):
        remote(agg_out.at[0], agg_in.at[k], agg_s.at[k], agg_r.at[k], partner).wait_recv()
        agg = agg + agg_in[k].astype(F32)
    gate = jax.nn.sigmoid(agg)
    hid = (upstream * gate * (1.0 + agg * (1.0 - gate))).astype(BF16)
    act = (agg * gate).astype(BF16)
    hid_all[me] = hid
    act_all[me] = act
    hid_ref[...] = hid
    for k in range(1, plane):
        c = remote(hid_all.at[me], hid_all.at[me], hid_s.at[k], hid_r.at[k], in_plane(k)[1])
        c.start()
        sent.append(c)
    for k in range(1, plane):
        c = remote(act_all.at[me], act_all.at[me], act_s.at[k], act_r.at[k], in_plane(k)[1])
        c.start()
        sent.append(c)

    b_copy.wait()
    b_sum = (b16.astype(F32) + b_in[...].astype(F32)).astype(BF16)
    for k in range(1, plane):
        q = before(k)
        remote(hid_all.at[q], hid_all.at[q], hid_s.at[k], hid_r.at[k], partner).wait_recv()
    lanes = pl.ds(pl.multiple_of(core * half, half), half)
    hid_half = hid_all[:, :, lanes].reshape(plane * own, half)
    gf = lax.dot_general(b_sum, hid_half, TN, preferred_element_type=F32)
    gf_z[z] = gf.astype(BF16)
    for k in range(1, reps):
        c = remote(gf_z.at[z], gf_z.at[z], gfz_s.at[k], gfz_r.at[k], in_z(k)[1])
        c.start()
        sent.append(c)
    for k in range(1, plane):
        q = before(k)
        remote(cot_ref, cot_all.at[q], cot_s.at[k], cot_r.at[k], partner).wait_recv()
    for k in range(1, plane):
        q = before(k)
        remote(act_all.at[q], act_all.at[q], act_s.at[k], act_r.at[k], partner).wait_recv()
    gu = lax.dot_general(
        act_all[...].reshape(plane * own, width), cot_all[...].reshape(plane * own, width), TN,
        preferred_element_type=F32,
    )
    gu_all[...] = gu.astype(BF16).reshape(gu_all.shape)
    gu_z[z] = gu_all[me]
    for k in range(1, reps):
        c = remote(gu_z.at[z], gu_z.at[z], guz_s.at[k], guz_r.at[k], in_z(k)[1])
        c.start()
        sent.append(c)
    for k in range(1, reps):
        q = before_z(k)
        remote(gf_z.at[q], gf_z.at[q], gfz_s.at[k], gfz_r.at[k], partner).wait_recv()
    gf_sum = gf_z[0].astype(F32)
    for q in range(1, reps):
        gf_sum = gf_sum + gf_z[q].astype(F32)
    gf_halves[core] = gf_sum.astype(BF16)
    c = remote(gf_halves.at[core], gf_halves.at[core], gfh_s, gfh_r, partner)
    c.start()
    sent.append(c)
    for k in range(1, reps):
        q = before_z(k)
        remote(gu_z.at[q], gu_z.at[q], guz_s.at[k], guz_r.at[k], partner).wait_recv()
    gu_sum = gu_z[0].astype(F32)
    for q in range(1, reps):
        gu_sum = gu_sum + gu_z[q].astype(F32)
    gu_ref[me] = gu_sum.astype(BF16)
    for k in range(1, plane):
        c = remote(gu_ref.at[me], gu_ref.at[me], gua_s.at[k], gua_r.at[k], in_plane(k)[1])
        c.start()
        sent.append(c)
    other = (core + 1) % sects
    remote(gf_halves.at[other], gf_halves.at[other], gfh_s, gfh_r, partner).wait_recv()
    for s in range(sects):
        gf_ref[:, s * half:(s + 1) * half] = gf_halves[s]
    for k in range(1, plane):
        q = before(k)
        remote(gu_ref.at[q], gu_ref.at[q], gua_s.at[k], gua_r.at[k], partner).wait_recv()
    for c in sent:
        c.wait_send()


def vmem():
    return pl.BlockSpec(memory_space=pltpu.VMEM)


def fast_step(axes, sizes, features, w_first, w_upper, cotangent, rows, cols, count, tiles):
    feats, sects, reps = sizes
    plane = feats * sects
    x = features[0]
    depth, src = x.shape
    slots, tile = tiles.shape[1], tiles.shape[2]
    own, width = cotangent.shape[1:]
    dst = own * plane
    half = width // sects
    smem = pl.BlockSpec(memory_space=pltpu.SMEM)
    hbm = pl.BlockSpec(memory_space=pl.ANY)
    mixed = pl.pallas_call(
        mix_kernel,
        out_shape=jax.ShapeDtypeStruct((dst, depth), BF16),
        in_specs=[smem, smem, smem, hbm, hbm],
        out_specs=vmem(),
        scratch_shapes=[
            pltpu.VMEM((dst, src), BF16),
            pltpu.VMEM((depth, src), BF16),
            pltpu.SemaphoreType.DMA((X_CHUNKS,)),
            pltpu.SemaphoreType.DMA((slots,)),
        ],
        name="mix",
    )(rows[0], cols[0], count[0], x, tiles[0])
    dma = pltpu.SemaphoreType.DMA
    hid, gf, gu = pl.pallas_call(
        functools.partial(exchange_kernel, axes, sizes),
        out_shape=(
            jax.ShapeDtypeStruct((own, width), BF16),
            jax.ShapeDtypeStruct((depth, width), BF16),
            jax.ShapeDtypeStruct((plane, width // plane, width), BF16),
        ),
        in_specs=[vmem()] * 4,
        out_specs=(vmem(), vmem(), vmem()),
        scratch_shapes=[
            pltpu.VMEM((plane, own, width), BF16),
            pltpu.VMEM((plane, own, width), BF16),
            pltpu.VMEM((plane, own, width), BF16),
            pltpu.VMEM((plane, own, width), BF16),
            pltpu.VMEM((plane, own, width), BF16),
            pltpu.VMEM((dst, depth), BF16),
            pltpu.VMEM((reps, depth, half), BF16),
            pltpu.VMEM((reps, width // plane, width), BF16),
            pltpu.VMEM((sects, depth, half), BF16),
            pltpu.VMEM((plane, width // plane, width), BF16),
            dma((plane,)), dma((plane,)), dma((plane,)), dma((plane,)),
            dma((plane,)), dma((plane,)), dma((plane,)), dma((plane,)),
            dma, dma,
            dma((reps,)), dma((reps,)), dma((reps,)), dma((reps,)),
            dma, dma,
            dma((plane,)), dma((plane,)),
        ],
        compiler_params=pltpu.CompilerParams(collective_id=0, has_side_effects=True),
        name="exchange",
    )(mixed, w_first, w_upper, cotangent[0])
    first_scale = 1.0 / math.sqrt(reps * sects * slots * tile)
    upper_scale = 1.0 / math.sqrt(reps * dst)
    return (
        hid[None],
        gf.astype(F32) * first_scale,
        gu.reshape(width, width).astype(F32) * upper_scale,
    )


def general_step(sizes, features, w_first, w_upper, cotangent, rows, cols, count, tiles):
    feats, sects, reps = sizes
    x = features[0]
    depth, src = x.shape
    slots, tile = tiles.shape[1], tiles.shape[2]
    own, width = cotangent.shape[1:]
    dst = own * feats * sects
    group = math.gcd(slots, 32)
    live = jnp.arange(slots, dtype=jnp.int32) < count[0, 0]
    grouped = (
        rows[0].reshape(-1, group),
        cols[0].reshape(-1, group),
        live.reshape(-1, group),
        tiles[0].reshape(-1, group, tile, tile),
    )
    x_blocks = x.reshape(depth, src // tile, tile).transpose(1, 0, 2)

    def body(running, inputs):
        r, c, alive, vals = inputs
        products = jnp.einsum("trc,tfc->trf", vals, x_blocks[c], preferred_element_type=F32)
        products = jnp.where(alive[:, None, None], products, 0.0)
        return running.at[r].add(products), None

    mixed = lax.scan(body, jnp.zeros((dst // tile, tile, depth), F32), grouped)[0]
    mixed = mixed.reshape(dst, depth).astype(BF16)
    part = jnp.dot(mixed, w_first, preferred_element_type=F32)
    agg = lax.psum_scatter(part, ("feat", "sect"), scatter_dimension=0, tiled=True)
    upstream = lax.dot_general(cotangent[0], w_upper, NT, preferred_element_type=F32)
    gate = jax.nn.sigmoid(agg)
    act = (agg * gate).astype(BF16)
    hid = (upstream * gate * (1.0 + agg * (1.0 - gate))).astype(BF16)
    upper = lax.dot_general(act, cotangent[0], TN, preferred_element_type=F32)
    grad_upper = lax.psum(upper, ("feat", "sect", "rep")) * (1.0 / math.sqrt(reps * dst))
    hid_all = lax.all_gather(hid, ("feat", "sect"), axis=0, tiled=True)
    first = lax.dot_general(mixed, hid_all, TN, preferred_element_type=F32)
    first_scale = 1.0 / math.sqrt(reps * sects * slots * tile)
    grad_first = lax.psum(first, ("sect", "rep")) * first_scale
    return hid[None], grad_first, grad_upper


def solution(mesh):
    axes = tuple(mesh.axis_names)
    sizes = tuple(mesh.shape[a] for a in ("feat", "sect", "rep"))
    plane = sizes[0] * sizes[1]
    small = plane <= 8 and sizes[1] == 2 and sizes[2] <= 4
    step = functools.partial(fast_step, axes, sizes) if small else functools.partial(general_step, sizes)
    in_specs = (
        P("rep", "feat", "sect"),
        P("feat", None),
        P(),
        P("rep", ("feat", "sect"), None),
        P("rep", "sect"),
        P("rep", "sect"),
        P("rep", "sect"),
        P("rep", "sect", None, None),
    )
    out_specs = (P("rep", ("feat", "sect"), None), P("feat", None), P())
    return jax.shard_map(step, mesh=mesh, in_specs=in_specs, out_specs=out_specs, check_vma=False)
```

```python
import functools
import math

import jax
import jax.numpy as jnp
from jax import lax
from jax.experimental import pallas as pl
from jax.experimental.pallas import tpu as pltpu
from jax.sharding import PartitionSpec as P

MESH = pl.DeviceIdType.MESH
F32 = jnp.float32
BF16 = jnp.bfloat16
NT = (((1,), (1,)), ((), ()))
TN = (((0,), (0,)), ((), ()))
LANES = 128
X_CHUNKS = 4


def mix_kernel(rows, cols, count, x_hbm, tiles_hbm, b_ref, dense, x_buf, x_sem, tile_sem):
    tile = tiles_hbm.shape[1]
    src = x_buf.shape[1]
    step = src // X_CHUNKS

    def x_copy(i):
        lanes = pl.ds(i * step, step)
        return pltpu.make_async_copy(x_hbm.at[:, lanes], x_buf.at[:, lanes], x_sem.at[i])

    for i in range(X_CHUNKS):
        x_copy(i).start()
    dense[...] = jnp.zeros_like(dense)

    def tile_copy(j):
        r = pl.multiple_of(rows[j] * tile, tile)
        c = pl.multiple_of(cols[j] * tile, tile)
        return pltpu.make_async_copy(
            tiles_hbm.at[j], dense.at[pl.ds(r, tile), pl.ds(c, tile)], tile_sem.at[j]
        )

    live = count[0, 0]

    def start(j, carry):
        tile_copy(j).start()
        return carry

    def finish(j, carry):
        tile_copy(j).wait()
        return carry

    lax.fori_loop(0, live, start, 0)
    lax.fori_loop(0, live, finish, 0)
    total = None
    for i in range(X_CHUNKS):
        x_copy(i).wait()
        lanes = pl.ds(i * step, step)
        part = lax.dot_general(dense[:, lanes], x_buf[:, lanes], NT, preferred_element_type=F32)
        total = part if total is None else total + part
    b_ref[...] = total


def exchange_kernel(
    axes, sizes, b_ref, wf_ref, wu_ref, cot_ref, hid_ref, gf_ref, gu_ref,
    b_own, b_in, cot_all, agg_out, agg_in, hid_cut, hid_all, act_cut, act_all,
    gf_out, gf_in, gu_cut, gu_z,
    cot_s, cot_r, agg_s, agg_r, hid_s, hid_r, act_s, act_r, b_s, b_r,
    gfz_s, gfz_r, guz_s, guz_r, gfa_s, gfa_r, gua_s, gua_r,
):
    feats, sects, reps = sizes
    plane, column = feats * sects, sects * reps
    pos = {a: lax.axis_index(a) for a in ("feat", "sect", "rep")}
    core, z = pos["sect"], pos["rep"]
    me = pos["feat"] * sects + core
    col = z * sects + core
    own, width = cot_ref.shape
    cut = width // plane
    per_cut = LANES // cut

    def dev(**changes):
        at = dict(pos, **changes)
        return tuple(at[a] for a in axes)

    def in_plane(k):
        q = (me + k) % plane
        return q, dev(feat=q // sects, sect=q % sects)

    def in_column(k):
        q = (col + k) % column
        return q, dev(rep=q // sects, sect=q % sects)

    def in_z(k):
        q = (z + k) % reps
        return q, dev(rep=q)

    partner = dev(sect=(core + 1) % sects)

    def remote(src, dst, s, r, to):
        return pltpu.make_async_remote_copy(
            src_ref=src, dst_ref=dst, send_sem=s, recv_sem=r, device_id=to, device_id_type=MESH
        )

    sent = []

    def send(src, dst, s, r, to):
        c = remote(src, dst, s, r, to)
        c.start()
        sent.append(c)

    barrier = pltpu.get_barrier_semaphore()
    for k in range(1, plane):
        pl.semaphore_signal(barrier, inc=1, device_id=in_plane(k)[1], device_id_type=MESH)
    for k in range(1, reps):
        for s in range(sects):
            to = dev(rep=(z + k) % reps, sect=s)
            pl.semaphore_signal(barrier, inc=1, device_id=to, device_id_type=MESH)

    cot_all[me] = cot_ref[...]
    upstream = lax.dot_general(cot_ref[...], wu_ref[...], NT, preferred_element_type=F32)
    b16 = b_ref[...].astype(BF16)
    b_own[...] = b16
    part = lax.dot_general(b16, wf_ref[...], (((1,), (0,)), ((), ())), preferred_element_type=F32)
    agg_out[...] = part.astype(BF16).reshape(agg_out.shape)
    pl.semaphore_wait(barrier, plane - 1 + (reps - 1) * sects)
    for k in range(1, plane):
        q, to = in_plane(k)
        send(agg_out.at[q], agg_in.at[k], agg_s.at[k], agg_r.at[k], to)
    send(b_own, b_in, b_s, b_r, partner)
    for k in range(1, plane):
        send(cot_ref, cot_all.at[me], cot_s.at[k], cot_r.at[k], in_plane(k)[1])

    agg = agg_out[me].astype(F32)
    for k in range(1, plane):
        remote(agg_out.at[0], agg_in.at[k], agg_s.at[k], agg_r.at[k], partner).wait_recv()
        agg = agg + agg_in[k].astype(F32)
    gate = jax.nn.sigmoid(agg)
    hid = (upstream * gate * (1.0 + agg * (1.0 - gate))).astype(BF16)
    act = (agg * gate).astype(BF16)
    for g in range(width // LANES):
        hid_cut[g] = hid[:, g * LANES:(g + 1) * LANES]
        act_cut[g] = act[:, g * LANES:(g + 1) * LANES]
    hid_all[me] = hid_cut[core]
    act_all[me] = act_cut[me // per_cut]
    for k in range(1, plane):
        q, to = in_plane(k)
        send(hid_cut.at[q % sects], hid_all.at[me], hid_s.at[k], hid_r.at[k], to)
    for k in range(1, plane):
        q, to = in_plane(k)
        send(act_cut.at[q // per_cut], act_all.at[me], act_s.at[k], act_r.at[k], to)
    hid_ref[...] = hid

    remote(b_own, b_in, b_s, b_r, partner).wait_recv()
    b_t = jnp.transpose(b_ref[...] + b_in[...].astype(F32)).astype(BF16)
    for k in range(1, plane):
        q = (me + plane - k) % plane
        remote(hid_cut.at[0], hid_all.at[q], hid_s.at[k], hid_r.at[k], partner).wait_recv()
    gf = jnp.dot(b_t, hid_all[...].reshape(plane * own, LANES), preferred_element_type=F32)
    gf_out[...] = gf.astype(BF16).reshape(gf_out.shape)
    for k in range(1, reps):
        q, to = in_z(k)
        send(gf_out.at[q], gf_in.at[k], gfz_s.at[k], gfz_r.at[k], to)
    for k in range(1, plane):
        q = (me + plane - k) % plane
        remote(cot_ref, cot_all.at[q], cot_s.at[k], cot_r.at[k], partner).wait_recv()
    for k in range(1, plane):
        q = (me + plane - k) % plane
        remote(act_cut.at[0], act_all.at[q], act_s.at[k], act_r.at[k], partner).wait_recv()
    gu = lax.dot_general(
        act_all[...].reshape(plane * own, LANES), cot_all[...].reshape(plane * own, width), TN,
        preferred_element_type=F32,
    )
    gu_cut[...] = gu.astype(BF16).reshape(gu_cut.shape)
    gu_z[z] = gu_cut[me % per_cut]
    for k in range(1, reps):
        send(gu_z.at[z], gu_z.at[z], guz_s.at[k], guz_r.at[k], in_z(k)[1])

    gf_sum = gf_out[z].astype(F32)
    for k in range(1, reps):
        remote(gf_out.at[0], gf_in.at[k], gfz_s.at[k], gfz_r.at[k], partner).wait_recv()
        gf_sum = gf_sum + gf_in[k].astype(F32)
    gf_ref[col] = gf_sum.astype(BF16)
    for k in range(1, column):
        send(gf_ref.at[col], gf_ref.at[col], gfa_s.at[k], gfa_r.at[k], in_column(k)[1])
    for k in range(1, reps):
        q = (z + reps - k) % reps
        remote(gu_z.at[q], gu_z.at[q], guz_s.at[k], guz_r.at[k], partner).wait_recv()
    gu_sum = gu_z[0].astype(F32)
    for q in range(1, reps):
        gu_sum = gu_sum + gu_z[q].astype(F32)
    gu_ref[me] = gu_sum.astype(BF16)
    for k in range(1, plane):
        send(gu_ref.at[me], gu_ref.at[me], gua_s.at[k], gua_r.at[k], in_plane(k)[1])
    for k in range(1, column):
        q = (col + column - k) % column
        remote(gf_ref.at[q], gf_ref.at[q], gfa_s.at[k], gfa_r.at[k], partner).wait_recv()
    for k in range(1, plane):
        q = (me + plane - k) % plane
        remote(gu_ref.at[q], gu_ref.at[q], gua_s.at[k], gua_r.at[k], partner).wait_recv()
    for c in sent:
        c.wait_send()


def finish_kernel(first_scale, upper_scale, sects, hid_in, gf_in, gu_in, hid_ref, gf_ref, gu_ref):
    hid_ref[...] = hid_in[...]
    n = gf_in.shape[1]
    for q in range(gf_in.shape[0]):
        r, s = q // sects, q % sects
        gf_ref[r * n:(r + 1) * n, s * LANES:(s + 1) * LANES] = gf_in[q].astype(F32) * first_scale
    m = gu_in.shape[1]
    for q in range(gu_in.shape[0]):
        gu_ref[q * m:(q + 1) * m, :] = gu_in[q].astype(F32) * upper_scale


def vmem():
    return pl.BlockSpec(memory_space=pltpu.VMEM)


def fast_step(axes, sizes, features, w_first, w_upper, cotangent, rows, cols, count, tiles):
    feats, sects, reps = sizes
    plane, column = feats * sects, sects * reps
    x = features[0]
    depth, src = x.shape
    slots, tile = tiles.shape[1], tiles.shape[2]
    own, width = cotangent.shape[1:]
    dst = own * plane
    cut = width // plane
    smem = pl.BlockSpec(memory_space=pltpu.SMEM)
    hbm = pl.BlockSpec(memory_space=pl.ANY)
    dma = pltpu.SemaphoreType.DMA
    first_scale = 1.0 / math.sqrt(reps * sects * slots * tile)
    upper_scale = 1.0 / math.sqrt(reps * dst)
    mixed = pl.pallas_call(
        mix_kernel,
        out_shape=pltpu.VMEM((dst, depth), F32),
        in_specs=[smem, smem, smem, hbm, hbm],
        out_specs=vmem(),
        scratch_shapes=[
            pltpu.VMEM((dst, src), BF16),
            pltpu.VMEM((depth, src), BF16),
            dma((X_CHUNKS,)),
            dma((slots,)),
        ],
        name="mix",
    )(rows[0], cols[0], count, x, tiles[0])
    parts = pl.pallas_call(
        functools.partial(exchange_kernel, axes, sizes),
        out_shape=(
            pltpu.VMEM((own, width), BF16),
            pltpu.VMEM((column, depth // reps, LANES), BF16),
            pltpu.VMEM((plane, cut, width), BF16),
        ),
        in_specs=[vmem()] * 4,
        out_specs=(vmem(), vmem(), vmem()),
        scratch_shapes=[
            pltpu.VMEM((dst, depth), BF16),
            pltpu.VMEM((dst, depth), BF16),
            pltpu.VMEM((plane, own, width), BF16),
            pltpu.VMEM((plane, own, width), BF16),
            pltpu.VMEM((plane, own, width), BF16),
            pltpu.VMEM((width // LANES, own, LANES), BF16),
            pltpu.VMEM((plane, own, LANES), BF16),
            pltpu.VMEM((width // LANES, own, LANES), BF16),
            pltpu.VMEM((plane, own, LANES), BF16),
            pltpu.VMEM((reps, depth // reps, LANES), BF16),
            pltpu.VMEM((reps, depth // reps, LANES), BF16),
            pltpu.VMEM((LANES // cut, cut, width), BF16),
            pltpu.VMEM((reps, cut, width), BF16),
            dma((plane,)), dma((plane,)), dma((plane,)), dma((plane,)),
            dma((plane,)), dma((plane,)), dma((plane,)), dma((plane,)),
            dma, dma,
            dma((reps,)), dma((reps,)), dma((reps,)), dma((reps,)),
            dma((column,)), dma((column,)), dma((plane,)), dma((plane,)),
        ],
        compiler_params=pltpu.CompilerParams(collective_id=0, has_side_effects=True),
        name="exchange",
    )(pltpu.with_memory_space_constraint(mixed, pltpu.VMEM), w_first, w_upper, cotangent[0])
    hid, gf, gu = pl.pallas_call(
        functools.partial(finish_kernel, first_scale, upper_scale, sects),
        out_shape=(
            jax.ShapeDtypeStruct((own, width), BF16),
            jax.ShapeDtypeStruct((depth, width), F32),
            jax.ShapeDtypeStruct((width, width), F32),
        ),
        in_specs=[vmem()] * 3,
        out_specs=(vmem(), vmem(), vmem()),
        name="finish",
    )(*[pltpu.with_memory_space_constraint(p, pltpu.VMEM) for p in parts])
    return hid[None], gf, gu


def general_step(sizes, features, w_first, w_upper, cotangent, rows, cols, count, tiles):
    feats, sects, reps = sizes
    x = features[0]
    depth, src = x.shape
    slots, tile = tiles.shape[1], tiles.shape[2]
    own, width = cotangent.shape[1:]
    dst = own * feats * sects
    group = math.gcd(slots, 32)
    live = jnp.arange(slots, dtype=jnp.int32) < count[0, 0]
    grouped = (
        rows[0].reshape(-1, group),
        cols[0].reshape(-1, group),
        live.reshape(-1, group),
        tiles[0].reshape(-1, group, tile, tile),
    )
    x_blocks = x.reshape(depth, src // tile, tile).transpose(1, 0, 2)

    def body(running, inputs):
        r, c, alive, vals = inputs
        products = jnp.einsum("trc,tfc->trf", vals, x_blocks[c], preferred_element_type=F32)
        products = jnp.where(alive[:, None, None], products, 0.0)
        return running.at[r].add(products), None

    mixed = lax.scan(body, jnp.zeros((dst // tile, tile, depth), F32), grouped)[0]
    mixed = mixed.reshape(dst, depth).astype(BF16)
    part = jnp.dot(mixed, w_first, preferred_element_type=F32)
    agg = lax.psum_scatter(part, ("feat", "sect"), scatter_dimension=0, tiled=True)
    upstream = lax.dot_general(cotangent[0], w_upper, NT, preferred_element_type=F32)
    gate = jax.nn.sigmoid(agg)
    act = (agg * gate).astype(BF16)
    hid = (upstream * gate * (1.0 + agg * (1.0 - gate))).astype(BF16)
    upper = lax.dot_general(act, cotangent[0], TN, preferred_element_type=F32)
    grad_upper = lax.psum(upper, ("feat", "sect", "rep")) * (1.0 / math.sqrt(reps * dst))
    hid_all = lax.all_gather(hid, ("feat", "sect"), axis=0, tiled=True)
    first = lax.dot_general(mixed, hid_all, TN, preferred_element_type=F32)
    first_scale = 1.0 / math.sqrt(reps * sects * slots * tile)
    grad_first = lax.psum(first, ("sect", "rep")) * first_scale
    return hid[None], grad_first, grad_upper


def solution(mesh):
    axes = tuple(mesh.axis_names)
    sizes = tuple(mesh.shape[a] for a in ("feat", "sect", "rep"))
    plane = sizes[0] * sizes[1]
    small = plane == 8 and sizes[1] == 2 and sizes[2] == 4
    step = functools.partial(fast_step, axes, sizes) if small else functools.partial(general_step, sizes)
    in_specs = (
        P("rep", "feat", "sect"),
        P("feat", None),
        P(),
        P("rep", ("feat", "sect"), None),
        P("rep", "sect"),
        P("rep", "sect"),
        P("rep", "sect"),
        P("rep", "sect", None, None),
    )
    out_specs = (P("rep", ("feat", "sect"), None), P("feat", None), P())
    return jax.shard_map(step, mesh=mesh, in_specs=in_specs, out_specs=out_specs, check_vma=False)
```

```python
import functools
import math

import jax
import jax.numpy as jnp
from jax import lax
from jax.experimental import pallas as pl
from jax.experimental.pallas import tpu as pltpu
from jax.sharding import PartitionSpec as P

MESH = pl.DeviceIdType.MESH
F32 = jnp.float32
BF16 = jnp.bfloat16
NT = (((1,), (1,)), ((), ()))
TN = (((0,), (0,)), ((), ()))
LANES = 128
GROUP = 8


def step_kernel(
    axes, sizes, rows, cols, count, x_hbm, tiles_hbm, wf_ref, wu_ref, cot_ref, hid_ref, gf_ref, gu_ref,
    x_buf, t_buf, b_acc, b_own, b_in, cot_all, agg_out, agg_in, hid_cut, hid_all, act_cut, act_all,
    gf_out, gf_in, gu_cut, gu_z,
    x_sem, t_sem, cot_s, cot_r, agg_s, agg_r, hid_s, hid_r, act_s, act_r, b_s, b_r,
    gfz_s, gfz_r, guz_s, guz_r, gfa_s, gfa_r, gua_s, gua_r,
):
    feats, sects, reps = sizes
    plane, column = feats * sects, sects * reps
    pos = {a: lax.axis_index(a) for a in ("feat", "sect", "rep")}
    core, z = pos["sect"], pos["rep"]
    me = pos["feat"] * sects + core
    col = z * sects + core
    own, width = cot_ref.shape
    slots, tile = t_buf.shape[0], t_buf.shape[1]
    blocks = b_own.shape[0] // tile
    cut = width // plane
    per_cut = LANES // cut

    def dev(**changes):
        at = dict(pos, **changes)
        return tuple(at[a] for a in axes)

    def in_plane(k):
        q = (me + k) % plane
        return q, dev(feat=q // sects, sect=q % sects)

    def in_column(k):
        q = (col + k) % column
        return q, dev(rep=q // sects, sect=q % sects)

    def in_z(k):
        q = (z + k) % reps
        return q, dev(rep=q)

    partner = dev(sect=(core + 1) % sects)

    def remote(src, dst, s, r, to):
        return pltpu.make_async_remote_copy(
            src_ref=src, dst_ref=dst, send_sem=s, recv_sem=r, device_id=to, device_id_type=MESH
        )

    sent = []

    def send(src, dst, s, r, to):
        c = remote(src, dst, s, r, to)
        c.start()
        sent.append(c)

    barrier = pltpu.get_barrier_semaphore()
    for k in range(1, plane):
        pl.semaphore_signal(barrier, inc=1, device_id=in_plane(k)[1], device_id_type=MESH)
    for k in range(1, reps):
        for s in range(sects):
            to = dev(rep=(z + k) % reps, sect=s)
            pl.semaphore_signal(barrier, inc=1, device_id=to, device_id_type=MESH)

    def x_copy(i):
        lanes = pl.ds(pl.multiple_of(i * tile, tile), tile)
        return pltpu.make_async_copy(x_hbm.at[:, lanes], x_buf.at[i], x_sem.at[i])

    def t_copy(i):
        part = pl.ds(i * GROUP, GROUP)
        return pltpu.make_async_copy(tiles_hbm.at[part], t_buf.at[part], t_sem.at[i])

    for i in range(x_buf.shape[0]):
        x_copy(i).start()
    for i in range(slots // GROUP):
        t_copy(i).start()
    cot_all[me] = cot_ref[...]
    upstream = lax.dot_general(cot_ref[...], wu_ref[...], NT, preferred_element_type=F32)
    b_acc[...] = jnp.zeros_like(b_acc)
    pl.semaphore_wait(barrier, plane - 1 + (reps - 1) * sects)
    for k in range(1, plane):
        send(cot_ref, cot_all.at[me], cot_s.at[k], cot_r.at[k], in_plane(k)[1])
    for i in range(x_buf.shape[0]):
        x_copy(i).wait()

    live = count[0, 0]

    def mix(i, carry):
        t_copy(i).wait()
        left, right = [], []
        for n in range(GROUP):
            j = i * GROUP + n
            vals = t_buf[j]
            row, alive = rows[j], jnp.clip(live - j, 0, 1)
            kept = []
            for b in range(blocks):
                keep = (alive * (1 - jnp.minimum(jnp.abs(row - b), 1))).astype(F32)
                kept.append(vals * jnp.full(vals.shape, keep, F32).astype(BF16))
            left.append(jnp.concatenate(kept, axis=0))
            right.append(x_buf[cols[j]])
        b_acc[...] += lax.dot_general(
            jnp.concatenate(left, axis=1), jnp.concatenate(right, axis=1), NT,
            preferred_element_type=F32,
        )
        return carry

    lax.fori_loop(0, slots // GROUP, mix, 0)
    b16 = b_acc[...].astype(BF16)
    b_own[...] = b16
    part = lax.dot_general(b16, wf_ref[...], (((1,), (0,)), ((), ())), preferred_element_type=F32)
    agg_out[...] = part.astype(BF16).reshape(agg_out.shape)
    for k in range(1, plane):
        q, to = in_plane(k)
        send(agg_out.at[q], agg_in.at[k], agg_s.at[k], agg_r.at[k], to)
    send(b_own, b_in, b_s, b_r, partner)

    agg = agg_out[me].astype(F32)
    for k in range(1, plane):
        remote(agg_out.at[0], agg_in.at[k], agg_s.at[k], agg_r.at[k], partner).wait_recv()
        agg = agg + agg_in[k].astype(F32)
    gate = jax.nn.sigmoid(agg)
    hid = (upstream * gate * (1.0 + agg * (1.0 - gate))).astype(BF16)
    act = (agg * gate).astype(BF16)
    for g in range(width // LANES):
        hid_cut[g] = hid[:, g * LANES:(g + 1) * LANES]
        act_cut[g] = act[:, g * LANES:(g + 1) * LANES]
    hid_all[me] = hid_cut[core]
    act_all[me] = act_cut[me // per_cut]
    for k in range(1, plane):
        q, to = in_plane(k)
        send(hid_cut.at[q % sects], hid_all.at[me], hid_s.at[k], hid_r.at[k], to)
    for k in range(1, plane):
        q, to = in_plane(k)
        send(act_cut.at[q // per_cut], act_all.at[me], act_s.at[k], act_r.at[k], to)
    hid_ref[...] = hid

    remote(b_own, b_in, b_s, b_r, partner).wait_recv()
    b_t = jnp.transpose(b_acc[...] + b_in[...].astype(F32)).astype(BF16)
    for k in range(1, plane):
        q = (me + plane - k) % plane
        remote(hid_cut.at[0], hid_all.at[q], hid_s.at[k], hid_r.at[k], partner).wait_recv()
    gf = jnp.dot(b_t, hid_all[...].reshape(plane * own, LANES), preferred_element_type=F32)
    gf_out[...] = gf.astype(BF16).reshape(gf_out.shape)
    for k in range(1, reps):
        q, to = in_z(k)
        send(gf_out.at[q], gf_in.at[k], gfz_s.at[k], gfz_r.at[k], to)
    for k in range(1, plane):
        q = (me + plane - k) % plane
        remote(cot_ref, cot_all.at[q], cot_s.at[k], cot_r.at[k], partner).wait_recv()
    for k in range(1, plane):
        q = (me + plane - k) % plane
        remote(act_cut.at[0], act_all.at[q], act_s.at[k], act_r.at[k], partner).wait_recv()
    gu = lax.dot_general(
        act_all[...].reshape(plane * own, LANES), cot_all[...].reshape(plane * own, width), TN,
        preferred_element_type=F32,
    )
    gu_cut[...] = gu.astype(BF16).reshape(gu_cut.shape)
    gu_z[z] = gu_cut[me % per_cut]
    for k in range(1, reps):
        send(gu_z.at[z], gu_z.at[z], guz_s.at[k], guz_r.at[k], in_z(k)[1])

    gf_sum = gf_out[z].astype(F32)
    for k in range(1, reps):
        remote(gf_out.at[0], gf_in.at[k], gfz_s.at[k], gfz_r.at[k], partner).wait_recv()
        gf_sum = gf_sum + gf_in[k].astype(F32)
    gf_ref[col] = gf_sum.astype(BF16)
    for k in range(1, column):
        send(gf_ref.at[col], gf_ref.at[col], gfa_s.at[k], gfa_r.at[k], in_column(k)[1])
    for k in range(1, reps):
        q = (z + reps - k) % reps
        remote(gu_z.at[q], gu_z.at[q], guz_s.at[k], guz_r.at[k], partner).wait_recv()
    gu_sum = gu_z[0].astype(F32)
    for q in range(1, reps):
        gu_sum = gu_sum + gu_z[q].astype(F32)
    gu_ref[me] = gu_sum.astype(BF16)
    for k in range(1, plane):
        send(gu_ref.at[me], gu_ref.at[me], gua_s.at[k], gua_r.at[k], in_plane(k)[1])
    for k in range(1, column):
        q = (col + column - k) % column
        remote(gf_ref.at[q], gf_ref.at[q], gfa_s.at[k], gfa_r.at[k], partner).wait_recv()
    for k in range(1, plane):
        q = (me + plane - k) % plane
        remote(gu_ref.at[q], gu_ref.at[q], gua_s.at[k], gua_r.at[k], partner).wait_recv()
    for c in sent:
        c.wait_send()


def finish_kernel(first_scale, upper_scale, sects, hid_in, gf_in, gu_in, hid_ref, gf_ref, gu_ref):
    hid_ref[...] = hid_in[...]
    n = gf_in.shape[1]
    for q in range(gf_in.shape[0]):
        r, s = q // sects, q % sects
        gf_ref[r * n:(r + 1) * n, s * LANES:(s + 1) * LANES] = gf_in[q].astype(F32) * first_scale
    m = gu_in.shape[1]
    for q in range(gu_in.shape[0]):
        gu_ref[q * m:(q + 1) * m, :] = gu_in[q].astype(F32) * upper_scale


def vmem():
    return pl.BlockSpec(memory_space=pltpu.VMEM)


def fast_step(axes, sizes, features, w_first, w_upper, cotangent, rows, cols, count, tiles):
    feats, sects, reps = sizes
    plane, column = feats * sects, sects * reps
    x = features[0]
    depth, src = x.shape
    slots, tile = tiles.shape[1], tiles.shape[2]
    own, width = cotangent.shape[1:]
    dst = own * plane
    cut = width // plane
    smem = pl.BlockSpec(memory_space=pltpu.SMEM)
    hbm = pl.BlockSpec(memory_space=pl.ANY)
    dma = pltpu.SemaphoreType.DMA
    first_scale = 1.0 / math.sqrt(reps * sects * slots * tile)
    upper_scale = 1.0 / math.sqrt(reps * dst)
    parts = pl.pallas_call(
        functools.partial(step_kernel, axes, sizes),
        out_shape=(
            pltpu.VMEM((own, width), BF16),
            pltpu.VMEM((column, depth // reps, LANES), BF16),
            pltpu.VMEM((plane, cut, width), BF16),
        ),
        in_specs=[smem, smem, smem, hbm, hbm, vmem(), vmem(), vmem()],
        out_specs=(vmem(), vmem(), vmem()),
        scratch_shapes=[
            pltpu.VMEM((src // tile, depth, tile), BF16),
            pltpu.VMEM((slots, tile, tile), BF16),
            pltpu.VMEM((dst, depth), F32),
            pltpu.VMEM((dst, depth), BF16),
            pltpu.VMEM((dst, depth), BF16),
            pltpu.VMEM((plane, own, width), BF16),
            pltpu.VMEM((plane, own, width), BF16),
            pltpu.VMEM((plane, own, width), BF16),
            pltpu.VMEM((width // LANES, own, LANES), BF16),
            pltpu.VMEM((plane, own, LANES), BF16),
            pltpu.VMEM((width // LANES, own, LANES), BF16),
            pltpu.VMEM((plane, own, LANES), BF16),
            pltpu.VMEM((reps, depth // reps, LANES), BF16),
            pltpu.VMEM((reps, depth // reps, LANES), BF16),
            pltpu.VMEM((LANES // cut, cut, width), BF16),
            pltpu.VMEM((reps, cut, width), BF16),
            dma((src // tile,)), dma((slots // GROUP,)),
            dma((plane,)), dma((plane,)), dma((plane,)), dma((plane,)),
            dma((plane,)), dma((plane,)), dma((plane,)), dma((plane,)),
            dma, dma,
            dma((reps,)), dma((reps,)), dma((reps,)), dma((reps,)),
            dma((column,)), dma((column,)), dma((plane,)), dma((plane,)),
        ],
        compiler_params=pltpu.CompilerParams(collective_id=0, has_side_effects=True),
        name="step",
    )(rows[0], cols[0], count, x, tiles[0], w_first, w_upper, cotangent[0])
    hid, gf, gu = pl.pallas_call(
        functools.partial(finish_kernel, first_scale, upper_scale, sects),
        out_shape=(
            jax.ShapeDtypeStruct((own, width), BF16),
            jax.ShapeDtypeStruct((depth, width), F32),
            jax.ShapeDtypeStruct((width, width), F32),
        ),
        in_specs=[vmem()] * 3,
        out_specs=(vmem(), vmem(), vmem()),
        name="finish",
    )(*[pltpu.with_memory_space_constraint(p, pltpu.VMEM) for p in parts])
    return hid[None], gf, gu


def general_step(sizes, features, w_first, w_upper, cotangent, rows, cols, count, tiles):
    feats, sects, reps = sizes
    x = features[0]
    depth, src = x.shape
    slots, tile = tiles.shape[1], tiles.shape[2]
    own, width = cotangent.shape[1:]
    dst = own * feats * sects
    group = math.gcd(slots, 32)
    live = jnp.arange(slots, dtype=jnp.int32) < count[0, 0]
    grouped = (
        rows[0].reshape(-1, group),
        cols[0].reshape(-1, group),
        live.reshape(-1, group),
        tiles[0].reshape(-1, group, tile, tile),
    )
    x_blocks = x.reshape(depth, src // tile, tile).transpose(1, 0, 2)

    def body(running, inputs):
        r, c, alive, vals = inputs
        products = jnp.einsum("trc,tfc->trf", vals, x_blocks[c], preferred_element_type=F32)
        products = jnp.where(alive[:, None, None], products, 0.0)
        return running.at[r].add(products), None

    mixed = lax.scan(body, jnp.zeros((dst // tile, tile, depth), F32), grouped)[0]
    mixed = mixed.reshape(dst, depth).astype(BF16)
    part = jnp.dot(mixed, w_first, preferred_element_type=F32)
    agg = lax.psum_scatter(part, ("feat", "sect"), scatter_dimension=0, tiled=True)
    upstream = lax.dot_general(cotangent[0], w_upper, NT, preferred_element_type=F32)
    gate = jax.nn.sigmoid(agg)
    act = (agg * gate).astype(BF16)
    hid = (upstream * gate * (1.0 + agg * (1.0 - gate))).astype(BF16)
    upper = lax.dot_general(act, cotangent[0], TN, preferred_element_type=F32)
    grad_upper = lax.psum(upper, ("feat", "sect", "rep")) * (1.0 / math.sqrt(reps * dst))
    hid_all = lax.all_gather(hid, ("feat", "sect"), axis=0, tiled=True)
    first = lax.dot_general(mixed, hid_all, TN, preferred_element_type=F32)
    first_scale = 1.0 / math.sqrt(reps * sects * slots * tile)
    grad_first = lax.psum(first, ("sect", "rep")) * first_scale
    return hid[None], grad_first, grad_upper


def solution(mesh):
    axes = tuple(mesh.axis_names)
    sizes = tuple(mesh.shape[a] for a in ("feat", "sect", "rep"))
    plane = sizes[0] * sizes[1]
    small = plane == 8 and sizes[1] == 2 and sizes[2] == 4
    step = functools.partial(fast_step, axes, sizes) if small else functools.partial(general_step, sizes)
    in_specs = (
        P("rep", "feat", "sect"),
        P("feat", None),
        P(),
        P("rep", ("feat", "sect"), None),
        P("rep", "sect"),
        P("rep", "sect"),
        P("rep", "sect"),
        P("rep", "sect", None, None),
    )
    out_specs = (P("rep", ("feat", "sect"), None), P("feat", None), P())
    return jax.shard_map(step, mesh=mesh, in_specs=in_specs, out_specs=out_specs, check_vma=False)
```

```python
import functools
import math

import jax
import jax.numpy as jnp
from jax import lax
from jax.experimental import pallas as pl
from jax.experimental.pallas import tpu as pltpu
from jax.sharding import PartitionSpec as P

MESH = pl.DeviceIdType.MESH
F32 = jnp.float32
BF16 = jnp.bfloat16
NT = (((1,), (1,)), ((), ()))
TN = (((0,), (0,)), ((), ()))
LANES = 128
GROUP = 8


def step_kernel(
    axes, sizes, rows, cols, count, x_hbm, tiles_hbm, wf_ref, wu_ref, cot_ref, hid_ref, gf_ref, gu_ref,
    x_buf, t_buf, b_acc, b_own, b_in, cot_all, agg_out, agg_in, hid_cut, hid_all, act_cut, act_all,
    gf_out, gf_in, gu_cut, gu_z,
    x_sem, t_sem, cot_s, cot_r, agg_s, agg_r, hid_s, hid_r, act_s, act_r, b_s, b_r,
    gfz_s, gfz_r, guz_s, guz_r, gfa_s, gfa_r, gua_s, gua_r,
):
    feats, sects, reps = sizes
    plane, column = feats * sects, sects * reps
    pos = {a: lax.axis_index(a) for a in ("feat", "sect", "rep")}
    core, z = pos["sect"], pos["rep"]
    me = pos["feat"] * sects + core
    col = z * sects + core
    own, width = cot_ref.shape
    slots, tile = t_buf.shape[0], t_buf.shape[1]
    blocks = b_own.shape[0] // tile
    cut = width // plane
    per_cut = LANES // cut

    def dev(**changes):
        at = dict(pos, **changes)
        return tuple(at[a] for a in axes)

    feat = pos["feat"]
    chips = (feats - 1 - feat, feat + 1 - 2 * (feat % 2), (feat + feats // 2) % feats, feat)
    across = []
    for n, f in enumerate(chips):
        for s in range(sects):
            c = (core + 1 + s) % sects
            if n < len(chips) - 1 or s < sects - 1:
                q = f * sects + c
                across.append(((q + plane - me) % plane, q, c, dev(feat=f, sect=c)))
    upper = z // (reps // 2)
    along, over = [], []
    for t in range(1, reps):
        k = t + (1 - upper) * (reps - 2 * t)
        r = (z + k) % reps
        along.append((k, r, dev(rep=r)))
        for s in range(sects):
            q = r * sects + s
            over.append(((q + column - col) % column, dev(rep=r, sect=s)))
    over.append((((z * sects + (core + 1) % sects) + column - col) % column, dev(sect=(core + 1) % sects)))

    partner = dev(sect=(core + 1) % sects)

    def remote(src, dst, s, r, to):
        return pltpu.make_async_remote_copy(
            src_ref=src, dst_ref=dst, send_sem=s, recv_sem=r, device_id=to, device_id_type=MESH
        )

    sent = []

    def send(src, dst, s, r, to):
        c = remote(src, dst, s, r, to)
        c.start()
        sent.append(c)

    barrier = pltpu.get_barrier_semaphore()
    for _, to in over[:-1]:
        pl.semaphore_signal(barrier, inc=1, device_id=to, device_id_type=MESH)
    for _, _, _, to in across:
        pl.semaphore_signal(barrier, inc=1, device_id=to, device_id_type=MESH)

    def x_copy(i):
        lanes = pl.ds(pl.multiple_of(i * tile, tile), tile)
        return pltpu.make_async_copy(x_hbm.at[:, lanes], x_buf.at[i], x_sem.at[i])

    def t_copy(i):
        part = pl.ds(i * GROUP, GROUP)
        return pltpu.make_async_copy(tiles_hbm.at[part], t_buf.at[part], t_sem.at[i])

    for i in range(x_buf.shape[0]):
        x_copy(i).start()
    for i in range(slots // GROUP):
        t_copy(i).start()
    cot_all[me] = cot_ref[...]
    upstream = lax.dot_general(cot_ref[...], wu_ref[...], NT, preferred_element_type=F32)
    b_acc[...] = jnp.zeros_like(b_acc)
    pl.semaphore_wait(barrier, plane - 1 + (reps - 1) * sects)
    for k, _, _, to in across:
        send(cot_ref, cot_all.at[me], cot_s.at[k], cot_r.at[k], to)
    for i in range(x_buf.shape[0]):
        x_copy(i).wait()

    live = count[0, 0]

    def mix(i, carry):
        t_copy(i).wait()
        left, right = [], []
        for n in range(GROUP):
            j = i * GROUP + n
            vals = t_buf[j]
            row, alive = rows[j], jnp.clip(live - j, 0, 1)
            kept = []
            for b in range(blocks):
                keep = (alive * (1 - jnp.minimum(jnp.abs(row - b), 1))).astype(F32)
                kept.append(vals * jnp.full(vals.shape, keep, F32).astype(BF16))
            left.append(jnp.concatenate(kept, axis=0))
            right.append(x_buf[cols[j]])
        b_acc[...] += lax.dot_general(
            jnp.concatenate(left, axis=1), jnp.concatenate(right, axis=1), NT,
            preferred_element_type=F32,
        )
        return carry

    lax.fori_loop(0, slots // GROUP, mix, 0)
    b16 = b_acc[...].astype(BF16)
    b_own[...] = b16
    part = lax.dot_general(b16, wf_ref[...], (((1,), (0,)), ((), ())), preferred_element_type=F32)
    agg_out[...] = part.astype(BF16).reshape(agg_out.shape)
    for k, q, _, to in across:
        send(agg_out.at[q], agg_in.at[k], agg_s.at[k], agg_r.at[k], to)
    send(b_own, b_in, b_s, b_r, partner)

    agg = agg_out[me].astype(F32)
    for k in range(1, plane):
        remote(agg_out.at[0], agg_in.at[k], agg_s.at[k], agg_r.at[k], partner).wait_recv()
        agg = agg + agg_in[k].astype(F32)
    gate = jax.nn.sigmoid(agg)
    hid = (upstream * gate * (1.0 + agg * (1.0 - gate))).astype(BF16)
    act = (agg * gate).astype(BF16)
    for g in range(width // LANES):
        hid_cut[g] = hid[:, g * LANES:(g + 1) * LANES]
        act_cut[g] = act[:, g * LANES:(g + 1) * LANES]
    hid_all[me] = hid_cut[core]
    act_all[me] = act_cut[me // per_cut]
    for k, _, c, to in across:
        send(hid_cut.at[c], hid_all.at[me], hid_s.at[k], hid_r.at[k], to)
    for k, q, _, to in across:
        send(act_cut.at[q // per_cut], act_all.at[me], act_s.at[k], act_r.at[k], to)
    hid_ref[...] = hid

    remote(b_own, b_in, b_s, b_r, partner).wait_recv()
    b_t = jnp.transpose(b_acc[...] + b_in[...].astype(F32)).astype(BF16)
    for k in range(1, plane):
        q = (me + plane - k) % plane
        remote(hid_cut.at[0], hid_all.at[q], hid_s.at[k], hid_r.at[k], partner).wait_recv()
    gf = jnp.dot(b_t, hid_all[...].reshape(plane * own, LANES), preferred_element_type=F32)
    gf_out[...] = gf.astype(BF16).reshape(gf_out.shape)
    for k, q, to in along:
        send(gf_out.at[q], gf_in.at[k], gfz_s.at[k], gfz_r.at[k], to)
    for k in range(1, plane):
        q = (me + plane - k) % plane
        remote(cot_ref, cot_all.at[q], cot_s.at[k], cot_r.at[k], partner).wait_recv()
    for k in range(1, plane):
        q = (me + plane - k) % plane
        remote(act_cut.at[0], act_all.at[q], act_s.at[k], act_r.at[k], partner).wait_recv()
    gu = lax.dot_general(
        act_all[...].reshape(plane * own, LANES), cot_all[...].reshape(plane * own, width), TN,
        preferred_element_type=F32,
    )
    gu_cut[...] = gu.astype(BF16).reshape(gu_cut.shape)
    gu_z[z] = gu_cut[me % per_cut]
    for k, _, to in along:
        send(gu_z.at[z], gu_z.at[z], guz_s.at[k], guz_r.at[k], to)

    gf_sum = gf_out[z].astype(F32)
    for k in range(1, reps):
        remote(gf_out.at[0], gf_in.at[k], gfz_s.at[k], gfz_r.at[k], partner).wait_recv()
        gf_sum = gf_sum + gf_in[k].astype(F32)
    gf_ref[col] = gf_sum.astype(BF16)
    for k, to in over:
        send(gf_ref.at[col], gf_ref.at[col], gfa_s.at[k], gfa_r.at[k], to)
    for k in range(1, reps):
        q = (z + reps - k) % reps
        remote(gu_z.at[q], gu_z.at[q], guz_s.at[k], guz_r.at[k], partner).wait_recv()
    gu_sum = gu_z[0].astype(F32)
    for q in range(1, reps):
        gu_sum = gu_sum + gu_z[q].astype(F32)
    gu_ref[me] = gu_sum.astype(BF16)
    for k, _, _, to in across:
        send(gu_ref.at[me], gu_ref.at[me], gua_s.at[k], gua_r.at[k], to)
    for k in range(1, column):
        q = (col + column - k) % column
        remote(gf_ref.at[q], gf_ref.at[q], gfa_s.at[k], gfa_r.at[k], partner).wait_recv()
    for k in range(1, plane):
        q = (me + plane - k) % plane
        remote(gu_ref.at[q], gu_ref.at[q], gua_s.at[k], gua_r.at[k], partner).wait_recv()
    for c in sent:
        c.wait_send()


def finish_kernel(first_scale, upper_scale, sects, hid_in, gf_in, gu_in, hid_ref, gf_ref, gu_ref):
    hid_ref[...] = hid_in[...]
    n = gf_in.shape[1]
    for q in range(gf_in.shape[0]):
        r, s = q // sects, q % sects
        gf_ref[r * n:(r + 1) * n, s * LANES:(s + 1) * LANES] = gf_in[q].astype(F32) * first_scale
    m = gu_in.shape[1]
    for q in range(gu_in.shape[0]):
        gu_ref[q * m:(q + 1) * m, :] = gu_in[q].astype(F32) * upper_scale


def vmem():
    return pl.BlockSpec(memory_space=pltpu.VMEM)


def fast_step(axes, sizes, features, w_first, w_upper, cotangent, rows, cols, count, tiles):
    feats, sects, reps = sizes
    plane, column = feats * sects, sects * reps
    x = features[0]
    depth, src = x.shape
    slots, tile = tiles.shape[1], tiles.shape[2]
    own, width = cotangent.shape[1:]
    dst = own * plane
    cut = width // plane
    smem = pl.BlockSpec(memory_space=pltpu.SMEM)
    hbm = pl.BlockSpec(memory_space=pl.ANY)
    dma = pltpu.SemaphoreType.DMA
    first_scale = 1.0 / math.sqrt(reps * sects * slots * tile)
    upper_scale = 1.0 / math.sqrt(reps * dst)
    parts = pl.pallas_call(
        functools.partial(step_kernel, axes, sizes),
        out_shape=(
            pltpu.VMEM((own, width), BF16),
            pltpu.VMEM((column, depth // reps, LANES), BF16),
            pltpu.VMEM((plane, cut, width), BF16),
        ),
        in_specs=[smem, smem, smem, hbm, hbm, vmem(), vmem(), vmem()],
        out_specs=(vmem(), vmem(), vmem()),
        scratch_shapes=[
            pltpu.VMEM((src // tile, depth, tile), BF16),
            pltpu.VMEM((slots, tile, tile), BF16),
            pltpu.VMEM((dst, depth), F32),
            pltpu.VMEM((dst, depth), BF16),
            pltpu.VMEM((dst, depth), BF16),
            pltpu.VMEM((plane, own, width), BF16),
            pltpu.VMEM((plane, own, width), BF16),
            pltpu.VMEM((plane, own, width), BF16),
            pltpu.VMEM((width // LANES, own, LANES), BF16),
            pltpu.VMEM((plane, own, LANES), BF16),
            pltpu.VMEM((width // LANES, own, LANES), BF16),
            pltpu.VMEM((plane, own, LANES), BF16),
            pltpu.VMEM((reps, depth // reps, LANES), BF16),
            pltpu.VMEM((reps, depth // reps, LANES), BF16),
            pltpu.VMEM((LANES // cut, cut, width), BF16),
            pltpu.VMEM((reps, cut, width), BF16),
            dma((src // tile,)), dma((slots // GROUP,)),
            dma((plane,)), dma((plane,)), dma((plane,)), dma((plane,)),
            dma((plane,)), dma((plane,)), dma((plane,)), dma((plane,)),
            dma, dma,
            dma((reps,)), dma((reps,)), dma((reps,)), dma((reps,)),
            dma((column,)), dma((column,)), dma((plane,)), dma((plane,)),
        ],
        compiler_params=pltpu.CompilerParams(collective_id=0, has_side_effects=True),
        name="step",
    )(rows[0], cols[0], count, x, tiles[0], w_first, w_upper, cotangent[0])
    hid, gf, gu = pl.pallas_call(
        functools.partial(finish_kernel, first_scale, upper_scale, sects),
        out_shape=(
            jax.ShapeDtypeStruct((own, width), BF16),
            jax.ShapeDtypeStruct((depth, width), F32),
            jax.ShapeDtypeStruct((width, width), F32),
        ),
        in_specs=[vmem()] * 3,
        out_specs=(vmem(), vmem(), vmem()),
        name="finish",
    )(*[pltpu.with_memory_space_constraint(p, pltpu.VMEM) for p in parts])
    return hid[None], gf, gu


def general_step(sizes, features, w_first, w_upper, cotangent, rows, cols, count, tiles):
    feats, sects, reps = sizes
    x = features[0]
    depth, src = x.shape
    slots, tile = tiles.shape[1], tiles.shape[2]
    own, width = cotangent.shape[1:]
    dst = own * feats * sects
    group = math.gcd(slots, 32)
    live = jnp.arange(slots, dtype=jnp.int32) < count[0, 0]
    grouped = (
        rows[0].reshape(-1, group),
        cols[0].reshape(-1, group),
        live.reshape(-1, group),
        tiles[0].reshape(-1, group, tile, tile),
    )
    x_blocks = x.reshape(depth, src // tile, tile).transpose(1, 0, 2)

    def body(running, inputs):
        r, c, alive, vals = inputs
        products = jnp.einsum("trc,tfc->trf", vals, x_blocks[c], preferred_element_type=F32)
        products = jnp.where(alive[:, None, None], products, 0.0)
        return running.at[r].add(products), None

    mixed = lax.scan(body, jnp.zeros((dst // tile, tile, depth), F32), grouped)[0]
    mixed = mixed.reshape(dst, depth).astype(BF16)
    part = jnp.dot(mixed, w_first, preferred_element_type=F32)
    agg = lax.psum_scatter(part, ("feat", "sect"), scatter_dimension=0, tiled=True)
    upstream = lax.dot_general(cotangent[0], w_upper, NT, preferred_element_type=F32)
    gate = jax.nn.sigmoid(agg)
    act = (agg * gate).astype(BF16)
    hid = (upstream * gate * (1.0 + agg * (1.0 - gate))).astype(BF16)
    upper = lax.dot_general(act, cotangent[0], TN, preferred_element_type=F32)
    grad_upper = lax.psum(upper, ("feat", "sect", "rep")) * (1.0 / math.sqrt(reps * dst))
    hid_all = lax.all_gather(hid, ("feat", "sect"), axis=0, tiled=True)
    first = lax.dot_general(mixed, hid_all, TN, preferred_element_type=F32)
    first_scale = 1.0 / math.sqrt(reps * sects * slots * tile)
    grad_first = lax.psum(first, ("sect", "rep")) * first_scale
    return hid[None], grad_first, grad_upper


def solution(mesh):
    axes = tuple(mesh.axis_names)
    sizes = tuple(mesh.shape[a] for a in ("feat", "sect", "rep"))
    plane = sizes[0] * sizes[1]
    small = sizes[0] == 4 and sizes[1] == 2 and sizes[2] == 4
    step = functools.partial(fast_step, axes, sizes) if small else functools.partial(general_step, sizes)
    in_specs = (
        P("rep", "feat", "sect"),
        P("feat", None),
        P(),
        P("rep", ("feat", "sect"), None),
        P("rep", "sect"),
        P("rep", "sect"),
        P("rep", "sect"),
        P("rep", "sect", None, None),
    )
    out_specs = (P("rep", ("feat", "sect"), None), P("feat", None), P())
    return jax.shard_map(step, mesh=mesh, in_specs=in_specs, out_specs=out_specs, check_vma=False)
```
